32 devices in a mesh: px: 4 (over z), py: 8 (over y, x, core).
Axes of the slice: x: 2, y: 2, z: 4, core: 2. Of those that a mesh axis runs over, the one named last changes fastest.
Arguments:
- stiffness: float32 [9, 3, 3, 64, 1024], P(None, None, None, 'px', 'py'), may hold values from -3 to 9, as said below
- basis: float32 [32, 3, 64, 1024], P(None, None, 'px', 'py'), may hold values from -6 to 6
- current: float32 [3, 64, 1024], P(None, 'px', 'py'), may hold values from -12 to 12, as said below
Outputs:
- new_vectors: float32 [3, 3, 64, 1024], P(None, None, 'px', 'py')
- coefficients: float32 [3, 36], replicated
The draws below stay inside these ranges and needn't reach their ends.
Inputs may be any that keep to these rules, and one draw needn't show every extreme that they name: `stiffness`: diagonal blocks of the centre coupling dominate each row. `current`: entries of order one.
All inputs are finite; a program needn't handle non-finite values.
Results may differ from the reference program's by a relative error of at most 0.0003.
Values sent between devices are 32-bit elements; how exact they have to be, the bound alone decides.
A program may use at most 64 MiB of HBM per device.

```python
import jax
import jax.numpy as jnp
from jax import lax

PRIOR = 32
STEPS = 3
NX = 64
NY = 1024


def shared_vectors(key):
    base = jax.random.fold_in(key, 7)
    vectors = jnp.clip(jax.random.normal(jax.random.fold_in(base, 1), (PRIOR, 3, NX, NY), jnp.float32), -6.0, 6.0)
    mixing = 0.25 * jax.random.normal(jax.random.fold_in(base, 2), (PRIOR,), jnp.float32)
    noise = jnp.clip(jax.random.normal(jax.random.fold_in(base, 3), (3, NX, NY), jnp.float32), -6.0, 6.0)
    raw = jnp.einsum('m,mabc->abc', mixing, vectors) + noise
    raw = raw / jnp.sqrt(jnp.mean(raw * raw))
    return (vectors, jnp.clip(raw, -12.0, 12.0))


def draw_basis(key, part):
    return shared_vectors(key)[0]


def draw_current(key, part):
    return shared_vectors(key)[1]


def draw_stiffness(key, part):
    base = jax.random.fold_in(key, 11)
    coupling = 0.2 * jnp.clip(jax.random.normal(jax.random.fold_in(base, 1), (9, 3, 3, NX, NY), jnp.float32), -6.0, 6.0)
    spread = jnp.exp(jax.random.uniform(jax.random.fold_in(base, 2), (1, 1, 1, NX, NY), jnp.float32, -0.69, 0.69))
    diagonal = jax.random.uniform(jax.random.fold_in(base, 3), (3, NX, NY), jnp.float32, 3.0, 6.0)
    centre = jnp.eye(3, dtype=jnp.float32)[:, :, None, None] * diagonal[None]
    coupling = coupling * spread
    return coupling.at[4].add(centre)


def setup_inputs(seed: int = 0) -> dict:
    key_of = jax.random.split(jax.random.key(seed), 4)
    return {
        "stiffness": draw_stiffness(jax.random.fold_in(key_of[3], 71), 0),
        "basis": draw_basis(jax.random.fold_in(key_of[3], 71), 0),
        "current": draw_current(jax.random.fold_in(key_of[3], 71), 0),
    }


EPSILON = 1e-06

def stencil(padded, stiffness):
    height = padded.shape[1] - 2
    breadth = padded.shape[2] - 2
    total = jnp.zeros((3, height, breadth), jnp.float32)
    for shift_x in range(3):
        for shift_y in range(3):
            shifted = padded[:, shift_x:shift_x + height, shift_y:shift_y + breadth]
            total = total + lax.optimization_barrier(jnp.sum(stiffness[shift_x * 3 + shift_y] * shifted[None], axis=1))
    return total

def reference(stiffness, basis, current):
    degrees = 3.0 * NX * NY
    listed = [current]
    vector = current
    records = []
    for step in range(STEPS):
        padded = jnp.pad(vector, ((0, 0), (1, 1), (1, 1)))
        image = stencil(padded, stiffness)
        on_basis = jnp.einsum('mabc,abc->m', basis, image, precision=lax.Precision.HIGHEST) / degrees
        on_new = jnp.stack([jnp.sum(member * image) for member in listed]) / degrees
        projected = image - jnp.einsum('m,mabc->abc', on_basis, basis, precision=lax.Precision.HIGHEST)
        for place in range(len(listed)):
            projected = projected - on_new[place] * listed[place]
        beta = jnp.sqrt(jnp.sum(projected * projected) / degrees + EPSILON)
        vector = projected / beta
        listed.append(vector)
        records.append(jnp.concatenate([on_basis, on_new, beta[None], jnp.zeros((STEPS - 1 - step,), jnp.float32)]))
    return (jnp.stack(listed[1:]), jnp.stack(records))
```

```python
import jax
import jax.numpy as jnp
from jax import lax
from jax.experimental import pallas as pl
from jax.experimental.pallas import tpu as pltpu
from jax.sharding import PartitionSpec as P

STEPS = 3
EPSILON = 1e-06
MESH = pl.DeviceIdType.MESH
HIGHEST = lax.Precision.HIGHEST

SENDS = (
    (0, 1, 0, 16),
    (0, -1, 16, 16),
    (1, 1, 32, 8),
    (1, -1, 40, 8),
    (-1, 1, 48, 8),
    (-1, -1, 56, 8),
    (1, 0, 64, 8),
    (-1, 0, 72, 8),
)
COLS = 64
HALO = 80
EXTRA = 96
SQUARE = 120


def iota(shape, dim):
    return lax.broadcasted_iota(jnp.int32, shape, dim)


def kernel(
    count, total_size,
    stiff_hbm, basis_hbm, cur_hbm,
    new_out, coef_out,
    stiff, basis, fld, img, edge, halo_in, halo, vcols, vrows, vh_cols, vh_rows,
    parts, msg, recv,
    load_sem, halo_send, halo_recv, vh_send, vh_recv, msg_send, msg_recv,
):
    nx, ny = lax.axis_size("px"), lax.axis_size("py")
    n = nx * ny
    x, y = lax.axis_index("px"), lax.axis_index("py")
    me = x * ny + y
    rows, width = 16, 128
    fields = 3 * count

    load_cur = pltpu.make_async_copy(cur_hbm, fld.at[0], load_sem.at[0])
    load_basis = pltpu.make_async_copy(basis_hbm, basis, load_sem.at[1])
    load_stiff = pltpu.make_async_copy(stiff_hbm, stiff, load_sem.at[2])
    load_cur.start()
    load_stiff.start()
    load_basis.start()

    halo_in[...] = jnp.zeros_like(halo_in)
    vh_cols[...] = jnp.zeros_like(vh_cols)
    vh_rows[...] = jnp.zeros_like(vh_rows)
    parts[...] = jnp.zeros_like(parts)

    def peer_id(k):
        peer = lax.rem(me + k, n)
        return (lax.div(peer, ny), lax.rem(peer, ny))

    barrier = pltpu.get_barrier_semaphore()

    def greet(k, carry):
        pl.semaphore_signal(barrier, inc=1, device_id=peer_id(k), device_id_type=MESH)
        return carry

    lax.fori_loop(1, n, greet, 0)

    row16, lane16 = iota((rows, width), 0), iota((rows, width), 1)
    row8, lane8 = iota((8, width), 0), iota((8, width), 1)

    def pack_edges(read, slot):
        packed = jnp.zeros((rows, width), jnp.float32)
        lines = jnp.zeros((8, width), jnp.float32)
        for a in range(3):
            f = read(a)
            packed = jnp.where(lane16 == a, pltpu.roll(f, a + 1, 1), packed)
            packed = jnp.where(lane16 == 3 + a, pltpu.roll(f, 3 + a, 1), packed)
            lines = jnp.where(row8 == a, jnp.broadcast_to(f[rows - 1 :, :], (8, width)), lines)
            lines = jnp.where(row8 == 3 + a, jnp.broadcast_to(f[0:1, :], (8, width)), lines)
        edge[slot, 0:rows, :] = packed
        edge[slot, rows : rows + 8, :] = lines

    def present(dx, dy):
        return (x + dx >= 0) & (x + dx < nx) & (y + dy >= 0) & (y + dy < ny)

    def halo_copy(slot, i):
        dx, dy, at, size = SENDS[i]
        first = rows if at >= COLS else (8 if dx == 1 else 0)
        return pltpu.make_async_remote_copy(
            src_ref=edge.at[slot, pl.ds(first, size), :],
            dst_ref=halo_in.at[slot, pl.ds(at, size), :],
            send_sem=halo_send.at[slot, i],
            recv_sem=halo_recv.at[slot, i],
            device_id=(x + dx, y + dy),
            device_id_type=MESH,
        )

    def vh_copy(i):
        dx, dy, at, size = SENDS[i]
        if at >= COLS:
            side = 0 if dx == 1 else 1
            src = vrows.at[side]
            dst = vh_rows.at[side, pl.ds(0, fields), :]
        else:
            side = 0 if dy == 1 else 1
            src = vcols.at[side, pl.ds(8 if dx == 1 else 0, size), :]
            dst = vh_cols.at[pl.ds(at, size), :]
        return pltpu.make_async_remote_copy(
            src_ref=src, dst_ref=dst, send_sem=vh_send.at[i], recv_sem=vh_recv.at[i],
            device_id=(x + dx, y + dy), device_id_type=MESH,
        )

    def start_all(make):
        for i, (dx, dy, _, _) in enumerate(SENDS):
            @pl.when(present(dx, dy))
            def _():
                make(i).start()

    def wait_recv_all(make):
        for i, (dx, dy, _, _) in enumerate(SENDS):
            @pl.when(present(-dx, -dy))
            def _():
                make(i).wait_recv()

    def wait_send_all(make):
        for i, (dx, dy, _, _) in enumerate(SENDS):
            @pl.when(present(dx, dy))
            def _():
                make(i).wait_send()

    load_cur.wait()
    pack_edges(lambda a: fld[0, a], 0)
    pl.semaphore_wait(barrier, n - 1)
    start_all(lambda i: halo_copy(0, i))

    load_basis.wait()
    vrows[0] = basis[pl.ds(rows - 1, fields, stride=rows), :]
    vrows[1] = basis[pl.ds(0, fields, stride=rows), :]
    last_cols = jnp.zeros((rows, width), jnp.float32)
    first_cols = jnp.zeros((rows, width), jnp.float32)
    for k in range(fields):
        f = basis[k * rows : (k + 1) * rows, :]
        last_cols = jnp.where(lane16 == k, pltpu.roll(f, (k + 1) % width, 1), last_cols)
        first_cols = jnp.where(lane16 == k, pltpu.roll(f, k, 1) if k else f, first_cols)
    vcols[0] = last_cols
    vcols[1] = first_cols
    start_all(vh_copy)
    load_stiff.wait()

    def message_copy(s, k):
        return pltpu.make_async_remote_copy(
            src_ref=msg.at[s, pl.ds(0, 1), :],
            dst_ref=recv.at[s, pl.ds(me, 1), :],
            send_sem=msg_send.at[s],
            recv_sem=msg_recv.at[s],
            device_id=peer_id(k),
            device_id_type=MESH,
        )

    def send_message(s):
        folded = parts[pl.ds(0, width, stride=8), :]
        for j in range(1, 8):
            folded = folded + parts[pl.ds(j, width, stride=8), :]
        sums = lax.dot_general(
            jnp.ones((8, width), jnp.float32), folded, (((1,), (1,)), ((), ())),
            precision=HIGHEST, preferred_element_type=jnp.float32,
        )
        msg[s] = sums
        recv[s, pl.ds(me, 1), :] = sums[0:1]

        def send(k, carry):
            message_copy(s, k).start()
            return carry

        lax.fori_loop(1, n, send, 0)

    def wait_message(s):
        pltpu.make_async_copy(
            recv.at[s, pl.ds(0, n - 1), :], recv.at[s, pl.ds(0, n - 1), :], msg_recv.at[s]
        ).wait()
        summed = jnp.sum(recv[s], axis=0, keepdims=True) / total_size
        return jnp.broadcast_to(summed, (8, width))

    def fold(values):
        total = values[0]
        for value in values[1:]:
            total = total + value
        return total[0:8] + total[8:16]

    def splat(row, lane):
        return jnp.broadcast_to(row[:, lane : lane + 1], (8, width))

    def twice(tile):
        return jnp.concatenate([tile, tile], axis=0)

    def stencil(s):
        left, right = halo[s, 0:16, :], halo[s, 16:32, :]

        def around(f, above, below):
            up = jnp.where(row16 == 0, jnp.broadcast_to(above, f.shape), pltpu.roll(f, 1, 0))
            down = jnp.where(row16 == rows - 1, jnp.broadcast_to(below, f.shape), pltpu.roll(f, rows - 1, 0))
            return (up, f, down)

        lefts = around(left, halo[s, 39:40, :], halo[s, 48:49, :])
        rights = around(right, halo[s, 47:48, :], halo[s, 56:57, :])
        image = [jnp.zeros((rows, width), jnp.float32) for _ in range(3)]
        for b in range(3):
            moved = around(fld[s, b], halo[s, 64 + b : 65 + b, :], halo[s, 75 + b : 76 + b, :])
            for i in range(3):
                f = moved[i]
                l = pltpu.roll(lefts[i], width - b, 1) if b else lefts[i]
                r = pltpu.roll(rights[i], width - 4 - b, 1)
                west = jnp.where(lane16 == 0, l, pltpu.roll(f, 1, 1))
                east = jnp.where(lane16 == width - 1, r, pltpu.roll(f, width - 1, 1))
                for j, g in enumerate((west, f, east)):
                    for a in range(3):
                        image[a] = image[a] + stiff[3 * i + j, a, b] * g
        return image

    wait_recv_all(lambda i: halo_copy(0, i))
    halo[0] = halo_in[0]

    rows_out = []
    betas = []
    for s in range(STEPS):
        image = stencil(s)
        for a in range(3):
            img[a] = image[a]
        if s < STEPS - 1:
            pack_edges(lambda a: img[a], s + 1)
            start_all(lambda i, s=s: halo_copy(s + 1, i))
        for m in range(count):
            part = fold([basis[(3 * m + a) * rows : (3 * m + a + 1) * rows, :] * img[a] for a in range(3)])
            for a in range(3):
                parts[(3 * m + a) * 8 : (3 * m + a + 1) * 8, :] = part
        for k in range(s + 1):
            parts[(EXTRA + k) * 8 : (EXTRA + k + 1) * 8, :] = fold([fld[k, a] * img[a] for a in range(3)])
        parts[SQUARE * 8 : SQUARE * 8 + 8, :] = fold([fld[s, a] * fld[s, a] for a in range(3)])
        send_message(s)
        if s == 0:
            wait_recv_all(vh_copy)
        if s < STEPS - 1:
            wait_recv_all(lambda i, s=s: halo_copy(s + 1, i))
        dots = wait_message(s)

        if s == 0:
            inverse = jnp.ones((8, width), jnp.float32)
        else:
            beta = jnp.sqrt(splat(dots, SQUARE) + EPSILON)
            betas.append(beta)
            inverse = 1.0 / beta
            for a in range(3):
                vector = fld[s, a] * twice(inverse)
                fld[s, a] = vector
                new_out[s - 1, a] = vector
            if s < STEPS - 1:
                halo[s] = halo[s] * inverse[0:1]
        weights = dots * inverse
        weights = jnp.where(lane8 == EXTRA + s, weights * inverse, weights)
        rows_out.append(weights)
        result = [img[a] * twice(inverse) for a in range(3)]
        for m in range(count):
            w = twice(splat(weights, 3 * m))
            for a in range(3):
                result[a] = result[a] - w * basis[(3 * m + a) * rows : (3 * m + a + 1) * rows, :]
        for k in range(s + 1):
            w = twice(splat(weights, EXTRA + k))
            for a in range(3):
                result[a] = result[a] - w * fld[k, a]
        for a in range(3):
            fld[s + 1, a] = result[a]
        if s < STEPS - 1:
            sub, lane = iota((width, width), 0), iota((width, width), 1)
            picks = (lax.rem(sub, 3) == lax.rem(lane, 3)) & (sub < 6) & (lane < fields)
            spread = jnp.where(picks, jnp.broadcast_to(weights[0:1], (width, width)), 0.0)
            cols = lax.dot_general(
                vh_cols[...], spread, (((1,), (1,)), ((), ())),
                precision=HIGHEST, preferred_element_type=jnp.float32,
            )
            lines = [
                jnp.dot(spread[0:8], vh_rows[side], precision=HIGHEST, preferred_element_type=jnp.float32)
                for side in range(2)
            ]
            ring = halo_in[s + 1] * inverse[0:1] - jnp.concatenate([cols] + lines, axis=0)
            for k in range(s + 1):
                ring = ring - splat(weights, EXTRA + k)[0:1] * halo[k]
            halo[s + 1] = ring

    parts[SQUARE * 8 : SQUARE * 8 + 8, :] = fold([fld[STEPS, a] * fld[STEPS, a] for a in range(3)])
    send_message(STEPS)
    sub, lane = iota((width, width), 0), iota((width, width), 1)
    gather = jnp.where((sub == 3 * lane) & (lane < count), 1.0, 0.0)
    gather = jnp.where((sub - EXTRA == lane - count) & (lane >= count) & (lane < count + STEPS), 1.0, gather)
    stacked = rows_out[0]
    for s in range(1, STEPS):
        stacked = jnp.where(row8 == s, rows_out[s], stacked)
    stacked = jnp.where((lane8 >= EXTRA) & (lane8 > EXTRA + row8), 0.0, stacked)
    table = jnp.dot(stacked, gather, precision=HIGHEST, preferred_element_type=jnp.float32)
    last = wait_message(STEPS)
    beta = jnp.sqrt(splat(last, SQUARE) + EPSILON)
    betas.append(beta)
    for a in range(3):
        new_out[STEPS - 1, a] = fld[STEPS, a] * twice(1.0 / beta)
    for s in range(STEPS):
        table = jnp.where((row8 == s) & (lane8 == count + 1 + s), betas[s], table)
    coef_out[...] = table[0:STEPS, 0 : count + STEPS + 1]

    for s in range(STEPS):
        wait_send_all(lambda i, s=s: halo_copy(s, i))
    wait_send_all(vh_copy)
    for s in range(STEPS + 1):
        pltpu.make_async_copy(
            recv.at[s, pl.ds(0, n - 1), :], recv.at[s, pl.ds(0, n - 1), :], msg_send.at[s]
        ).wait()


def per_device(stiffness, basis, current):
    count, _, rows, width = basis.shape
    assert (rows, width) == (16, 128) and 3 * count <= EXTRA
    n = lax.axis_size("px") * lax.axis_size("py")
    total_size = 3.0 * rows * width * n
    f32 = jnp.float32
    vmem = pltpu.VMEM
    dma = pltpu.SemaphoreType.DMA

    def body(*refs):
        kernel(count, total_size, *refs)

    return pl.pallas_call(
        body,
        out_shape=(
            jax.ShapeDtypeStruct((STEPS, 3, rows, width), f32),
            jax.ShapeDtypeStruct((STEPS, count + STEPS + 1), f32),
        ),
        in_specs=[pl.BlockSpec(memory_space=pl.ANY)] * 3,
        out_specs=(pl.BlockSpec(memory_space=vmem), pl.BlockSpec(memory_space=vmem)),
        scratch_shapes=[
            vmem(stiffness.shape, f32),
            vmem((3 * count * rows, width), f32),
            vmem((STEPS + 1, 3, rows, width), f32),
            vmem((3, rows, width), f32),
            vmem((STEPS, rows + 8, width), f32),
            vmem((STEPS, HALO, width), f32),
            vmem((STEPS, HALO, width), f32),
            vmem((2, rows, width), f32),
            vmem((2, 3 * count, width), f32),
            vmem((COLS, width), f32),
            vmem((2, width, width), f32),
            vmem((8 * width, width), f32),
            vmem((STEPS + 1, 8, width), f32),
            vmem((STEPS + 1, n, width), f32),
            dma((3,)),
            dma((STEPS, len(SENDS))),
            dma((STEPS, len(SENDS))),
            dma((len(SENDS),)),
            dma((len(SENDS),)),
            dma((STEPS + 1,)),
            dma((STEPS + 1,)),
        ],
        compiler_params=pltpu.CompilerParams(collective_id=0, has_side_effects=True),
        name="arnoldi",
    )(stiffness, basis.reshape(3 * count * rows, width), current)


def solution(mesh):
    in_specs = (P(None, None, None, "px", "py"), P(None, None, "px", "py"), P(None, "px", "py"))
    out_specs = (P(None, None, "px", "py"), P())
    return jax.shard_map(
        per_device, mesh=mesh, in_specs=in_specs, out_specs=out_specs, check_vma=False
    )
```

```python
import jax
import jax.numpy as jnp
from jax import lax
from jax.experimental import pallas as pl
from jax.experimental.pallas import tpu as pltpu
from jax.sharding import PartitionSpec as P

STEPS = 3
EPSILON = 1e-06
MESH = pl.DeviceIdType.MESH
HIGHEST = lax.Precision.HIGHEST

SENDS = (
    (0, 1, 0, 16),
    (0, -1, 16, 16),
    (1, 1, 32, 8),
    (1, -1, 40, 8),
    (-1, 1, 48, 8),
    (-1, -1, 56, 8),
    (1, 0, 64, 8),
    (-1, 0, 72, 8),
)
COLS = 64
HALO = 80
EXTRA = 96
SQUARE = 120


def iota(shape, dim):
    return lax.broadcasted_iota(jnp.int32, shape, dim)


def kernel(
    count, total_size,
    stiff_hbm, basis_hbm, cur_hbm,
    new_out, coef_out,
    stiff, basis, fld, img, edge, halo_in, halo, vcols, vrows, vh_cols, vh_rows,
    parts, msg, recv,
    load_sem, halo_send, halo_recv, vh_send, vh_recv, msg_send, msg_recv,
):
    nx, ny = lax.axis_size("px"), lax.axis_size("py")
    n = nx * ny
    x, y = lax.axis_index("px"), lax.axis_index("py")
    me = x * ny + y
    rows, width = 16, 128
    fields = 3 * count

    load_cur = pltpu.make_async_copy(cur_hbm, fld.at[0], load_sem.at[0])
    load_basis = pltpu.make_async_copy(basis_hbm, basis, load_sem.at[1])
    load_stiff = pltpu.make_async_copy(stiff_hbm, stiff, load_sem.at[2])
    load_cur.start()
    load_stiff.start()
    load_basis.start()

    halo_in[...] = jnp.zeros_like(halo_in)
    vh_cols[...] = jnp.zeros_like(vh_cols)
    vh_rows[...] = jnp.zeros_like(vh_rows)
    parts[...] = jnp.zeros_like(parts)

    def for_peers(act):
        def plane(px, first):
            def one(k, py):
                py = jnp.where(py == ny - 1, 0, py + 1)
                act((px, py))
                return py

            start = y if first else jnp.where(y == 0, ny - 1, y - 1)
            lax.fori_loop(first, ny, one, start, unroll=min(8, ny) if not first else 1)

        def other(k, px):
            px = jnp.where(px == nx - 1, 0, px + 1)
            plane(px, 0)
            return px

        lax.fori_loop(1, nx, other, x)
        plane(x, 1)

    barrier = pltpu.get_barrier_semaphore()

    for_peers(lambda peer: pl.semaphore_signal(barrier, inc=1, device_id=peer, device_id_type=MESH))

    row16, lane16 = iota((rows, width), 0), iota((rows, width), 1)
    row8, lane8 = iota((8, width), 0), iota((8, width), 1)

    def pack_edges(read, slot):
        packed = jnp.zeros((rows, width), jnp.float32)
        lines = jnp.zeros((8, width), jnp.float32)
        for a in range(3):
            f = read(a)
            packed = jnp.where(lane16 == a, pltpu.roll(f, a + 1, 1), packed)
            packed = jnp.where(lane16 == 3 + a, pltpu.roll(f, 3 + a, 1), packed)
            lines = jnp.where(row8 == a, jnp.broadcast_to(f[rows - 1 :, :], (8, width)), lines)
            lines = jnp.where(row8 == 3 + a, jnp.broadcast_to(f[0:1, :], (8, width)), lines)
        edge[slot, 0:rows, :] = packed
        edge[slot, rows : rows + 8, :] = lines

    def present(dx, dy):
        return (x + dx >= 0) & (x + dx < nx) & (y + dy >= 0) & (y + dy < ny)

    def halo_copy(slot, i):
        dx, dy, at, size = SENDS[i]
        first = rows if at >= COLS else (8 if dx == 1 else 0)
        return pltpu.make_async_remote_copy(
            src_ref=edge.at[slot, pl.ds(first, size), :],
            dst_ref=halo_in.at[slot, pl.ds(at, size), :],
            send_sem=halo_send.at[slot, i],
            recv_sem=halo_recv.at[slot, i],
            device_id=(x + dx, y + dy),
            device_id_type=MESH,
        )

    def vh_copy(i):
        dx, dy, at, size = SENDS[i]
        if at >= COLS:
            side = 0 if dx == 1 else 1
            src = vrows.at[side]
            dst = vh_rows.at[side, pl.ds(0, fields), :]
        else:
            side = 0 if dy == 1 else 1
            src = vcols.at[side, pl.ds(8 if dx == 1 else 0, size), :]
            dst = vh_cols.at[pl.ds(at, size), :]
        return pltpu.make_async_remote_copy(
            src_ref=src, dst_ref=dst, send_sem=vh_send.at[i], recv_sem=vh_recv.at[i],
            device_id=(x + dx, y + dy), device_id_type=MESH,
        )

    def start_all(make):
        for i, (dx, dy, _, _) in enumerate(SENDS):
            @pl.when(present(dx, dy))
            def _():
                make(i).start()

    def wait_recv_all(make):
        for i, (dx, dy, _, _) in enumerate(SENDS):
            @pl.when(present(-dx, -dy))
            def _():
                make(i).wait_recv()

    def wait_send_all(make):
        for i, (dx, dy, _, _) in enumerate(SENDS):
            @pl.when(present(dx, dy))
            def _():
                make(i).wait_send()

    load_cur.wait()
    pack_edges(lambda a: fld[0, a], 0)
    pl.semaphore_wait(barrier, n - 1)
    start_all(lambda i: halo_copy(0, i))

    load_basis.wait()
    vrows[0] = basis[pl.ds(rows - 1, fields, stride=rows), :]
    vrows[1] = basis[pl.ds(0, fields, stride=rows), :]
    last_cols = jnp.zeros((rows, width), jnp.float32)
    first_cols = jnp.zeros((rows, width), jnp.float32)
    for k in range(fields):
        f = basis[k * rows : (k + 1) * rows, :]
        last_cols = jnp.where(lane16 == k, pltpu.roll(f, (k + 1) % width, 1), last_cols)
        first_cols = jnp.where(lane16 == k, pltpu.roll(f, k, 1) if k else f, first_cols)
    vcols[0] = last_cols
    vcols[1] = first_cols
    start_all(vh_copy)
    load_stiff.wait()

    def message_copy(s, peer):
        return pltpu.make_async_remote_copy(
            src_ref=msg.at[s, pl.ds(0, 1), :],
            dst_ref=recv.at[s, pl.ds(me, 1), :],
            send_sem=msg_send.at[s],
            recv_sem=msg_recv.at[s],
            device_id=peer,
            device_id_type=MESH,
        )

    def send_message(s):
        folded = parts[pl.ds(0, width, stride=8), :]
        for j in range(1, 8):
            folded = folded + parts[pl.ds(j, width, stride=8), :]
        sums = lax.dot_general(
            jnp.ones((8, width), jnp.float32), folded, (((1,), (1,)), ((), ())),
            precision=HIGHEST, preferred_element_type=jnp.float32,
        )
        msg[s] = sums
        recv[s, pl.ds(me, 1), :] = sums[0:1]

        for_peers(lambda peer: message_copy(s, peer).start())

    def wait_message(s):
        pltpu.make_async_copy(
            recv.at[s, pl.ds(0, n - 1), :], recv.at[s, pl.ds(0, n - 1), :], msg_recv.at[s]
        ).wait()
        summed = jnp.sum(recv[s], axis=0, keepdims=True) / total_size
        return jnp.broadcast_to(summed, (8, width))

    def fold(values):
        total = values[0]
        for value in values[1:]:
            total = total + value
        return total[0:8] + total[8:16]

    def splat(row, lane):
        return jnp.broadcast_to(row[:, lane : lane + 1], (8, width))

    def twice(tile):
        return jnp.concatenate([tile, tile], axis=0)

    def stencil(s):
        left, right = halo[s, 0:16, :], halo[s, 16:32, :]

        def around(f, above, below):
            up = jnp.where(row16 == 0, jnp.broadcast_to(above, f.shape), pltpu.roll(f, 1, 0))
            down = jnp.where(row16 == rows - 1, jnp.broadcast_to(below, f.shape), pltpu.roll(f, rows - 1, 0))
            return (up, f, down)

        lefts = around(left, halo[s, 39:40, :], halo[s, 48:49, :])
        rights = around(right, halo[s, 47:48, :], halo[s, 56:57, :])
        image = [jnp.zeros((rows, width), jnp.float32) for _ in range(3)]
        for b in range(3):
            moved = around(fld[s, b], halo[s, 64 + b : 65 + b, :], halo[s, 75 + b : 76 + b, :])
            for i in range(3):
                f = moved[i]
                l = pltpu.roll(lefts[i], width - b, 1) if b else lefts[i]
                r = pltpu.roll(rights[i], width - 4 - b, 1)
                west = jnp.where(lane16 == 0, l, pltpu.roll(f, 1, 1))
                east = jnp.where(lane16 == width - 1, r, pltpu.roll(f, width - 1, 1))
                for j, g in enumerate((west, f, east)):
                    for a in range(3):
                        image[a] = image[a] + stiff[3 * i + j, a, b] * g
        return image

    wait_recv_all(lambda i: halo_copy(0, i))
    halo[0] = halo_in[0]

    rows_out = []
    betas = []
    for s in range(STEPS):
        image = stencil(s)
        for a in range(3):
            img[a] = image[a]
        if s < STEPS - 1:
            pack_edges(lambda a: img[a], s + 1)
            start_all(lambda i, s=s: halo_copy(s + 1, i))
        for m in range(count):
            part = fold([basis[(3 * m + a) * rows : (3 * m + a + 1) * rows, :] * img[a] for a in range(3)])
            for a in range(3):
                parts[(3 * m + a) * 8 : (3 * m + a + 1) * 8, :] = part
        for k in range(s + 1):
            parts[(EXTRA + k) * 8 : (EXTRA + k + 1) * 8, :] = fold([fld[k, a] * img[a] for a in range(3)])
        parts[SQUARE * 8 : SQUARE * 8 + 8, :] = fold([fld[s, a] * fld[s, a] for a in range(3)])
        send_message(s)
        if s == 0:
            wait_recv_all(vh_copy)
        if s < STEPS - 1:
            wait_recv_all(lambda i, s=s: halo_copy(s + 1, i))
        dots = wait_message(s)

        if s == 0:
            inverse = jnp.ones((8, width), jnp.float32)
        else:
            beta = jnp.sqrt(splat(dots, SQUARE) + EPSILON)
            betas.append(beta)
            inverse = 1.0 / beta
            for a in range(3):
                vector = fld[s, a] * twice(inverse)
                fld[s, a] = vector
                new_out[s - 1, a] = vector
            if s < STEPS - 1:
                halo[s] = halo[s] * inverse[0:1]
        weights = dots * inverse
        weights = jnp.where(lane8 == EXTRA + s, weights * inverse, weights)
        rows_out.append(weights)
        result = [img[a] * twice(inverse) for a in range(3)]
        for m in range(count):
            w = twice(splat(weights, 3 * m))
            for a in range(3):
                result[a] = result[a] - w * basis[(3 * m + a) * rows : (3 * m + a + 1) * rows, :]
        for k in range(s + 1):
            w = twice(splat(weights, EXTRA + k))
            for a in range(3):
                result[a] = result[a] - w * fld[k, a]
        for a in range(3):
            fld[s + 1, a] = result[a]
        if s < STEPS - 1:
            sub, lane = iota((width, width), 0), iota((width, width), 1)
            picks = (lax.rem(sub, 3) == lax.rem(lane, 3)) & (sub < 6) & (lane < fields)
            spread = jnp.where(picks, jnp.broadcast_to(weights[0:1], (width, width)), 0.0)
            cols = lax.dot_general(
                vh_cols[...], spread, (((1,), (1,)), ((), ())),
                precision=HIGHEST, preferred_element_type=jnp.float32,
            )
            lines = [
                jnp.dot(spread[0:8], vh_rows[side], precision=HIGHEST, preferred_element_type=jnp.float32)
                for side in range(2)
            ]
            ring = halo_in[s + 1] * inverse[0:1] - jnp.concatenate([cols] + lines, axis=0)
            for k in range(s + 1):
                ring = ring - splat(weights, EXTRA + k)[0:1] * halo[k]
            halo[s + 1] = ring

    parts[SQUARE * 8 : SQUARE * 8 + 8, :] = fold([fld[STEPS, a] * fld[STEPS, a] for a in range(3)])
    send_message(STEPS)
    sub, lane = iota((width, width), 0), iota((width, width), 1)
    gather = jnp.where((sub == 3 * lane) & (lane < count), 1.0, 0.0)
    gather = jnp.where((sub - EXTRA == lane - count) & (lane >= count) & (lane < count + STEPS), 1.0, gather)
    stacked = rows_out[0]
    for s in range(1, STEPS):
        stacked = jnp.where(row8 == s, rows_out[s], stacked)
    stacked = jnp.where((lane8 >= EXTRA) & (lane8 > EXTRA + row8), 0.0, stacked)
    table = jnp.dot(stacked, gather, precision=HIGHEST, preferred_element_type=jnp.float32)
    last = wait_message(STEPS)
    beta = jnp.sqrt(splat(last, SQUARE) + EPSILON)
    betas.append(beta)
    for a in range(3):
        new_out[STEPS - 1, a] = fld[STEPS, a] * twice(1.0 / beta)
    for s in range(STEPS):
        table = jnp.where((row8 == s) & (lane8 == count + 1 + s), betas[s], table)
    coef_out[...] = table[0:STEPS, 0 : count + STEPS + 1]

    for s in range(STEPS):
        wait_send_all(lambda i, s=s: halo_copy(s, i))
    wait_send_all(vh_copy)
    for s in range(STEPS + 1):
        pltpu.make_async_copy(
            recv.at[s, pl.ds(0, n - 1), :], recv.at[s, pl.ds(0, n - 1), :], msg_send.at[s]
        ).wait()


def per_device(stiffness, basis, current):
    count, _, rows, width = basis.shape
    assert (rows, width) == (16, 128) and 3 * count <= EXTRA
    n = lax.axis_size("px") * lax.axis_size("py")
    total_size = 3.0 * rows * width * n
    f32 = jnp.float32
    vmem = pltpu.VMEM
    dma = pltpu.SemaphoreType.DMA

    def body(*refs):
        kernel(count, total_size, *refs)

    new, coef = pl.pallas_call(
        body,
        out_shape=(
            jax.ShapeDtypeStruct((STEPS, 3, rows, width), f32),
            jax.ShapeDtypeStruct((STEPS, count + STEPS + 1), f32),
        ),
        in_specs=[pl.BlockSpec(memory_space=pl.ANY)] * 3,
        out_specs=(pl.BlockSpec(memory_space=vmem), pl.BlockSpec(memory_space=vmem)),
        scratch_shapes=[
            vmem(stiffness.shape, f32),
            vmem((3 * count * rows, width), f32),
            vmem((STEPS + 1, 3, rows, width), f32),
            vmem((3, rows, width), f32),
            vmem((STEPS, rows + 8, width), f32),
            vmem((STEPS, HALO, width), f32),
            vmem((STEPS, HALO, width), f32),
            vmem((2, rows, width), f32),
            vmem((2, 3 * count, width), f32),
            vmem((COLS, width), f32),
            vmem((2, width, width), f32),
            vmem((8 * width, width), f32),
            vmem((STEPS + 1, 8, width), f32),
            vmem((STEPS + 1, n, width), f32),
            dma((3,)),
            dma((STEPS, len(SENDS))),
            dma((STEPS, len(SENDS))),
            dma((len(SENDS),)),
            dma((len(SENDS),)),
            dma((STEPS + 1,)),
            dma((STEPS + 1,)),
        ],
        compiler_params=pltpu.CompilerParams(collective_id=0, has_side_effects=True),
        name="arnoldi",
    )(stiffness, basis.reshape(3 * count * rows, width), current)

    def hand_out(new_ref, coef_ref, new_out, coef_out):
        new_out[...] = new_ref[...]
        coef_out[...] = coef_ref[...]

    return pl.pallas_call(
        hand_out,
        out_shape=(
            jax.ShapeDtypeStruct(new.shape, f32),
            jax.ShapeDtypeStruct(coef.shape, f32),
        ),
        in_specs=[pl.BlockSpec(memory_space=vmem)] * 2,
        out_specs=(pl.BlockSpec(memory_space=vmem), pl.BlockSpec(memory_space=vmem)),
        name="hand_out",
    )(new, coef)


def solution(mesh):
    in_specs = (P(None, None, None, "px", "py"), P(None, None, "px", "py"), P(None, "px", "py"))
    out_specs = (P(None, None, "px", "py"), P())
    return jax.shard_map(
        per_device, mesh=mesh, in_specs=in_specs, out_specs=out_specs, check_vma=False
    )
```

```python
import jax
import jax.numpy as jnp
from jax import lax
from jax.experimental import pallas as pl
from jax.experimental.pallas import tpu as pltpu
from jax.sharding import PartitionSpec as P

STEPS = 3
EPSILON = 1e-06
MESH = pl.DeviceIdType.MESH
HIGHEST = lax.Precision.HIGHEST

SENDS = (
    (0, 1, 0, 16),
    (0, -1, 16, 16),
    (1, 1, 32, 8),
    (1, -1, 40, 8),
    (-1, 1, 48, 8),
    (-1, -1, 56, 8),
    (1, 0, 64, 8),
    (-1, 0, 72, 8),
)
COLS = 64
HALO = 80
EXTRA = 96
SQUARE = 120


def iota(shape, dim):
    return lax.broadcasted_iota(jnp.int32, shape, dim)


def kernel(
    count, total_size,
    stiff_hbm, basis_hbm, cur_hbm,
    new_out, coef_out,
    stiff, basis, fld, img, edge, halo_in, halo, vcols, vrows, vh_cols, vh_rows,
    parts, msg, recv,
    load_sem, halo_send, halo_recv, vh_send, vh_recv, msg_send, msg_recv,
):
    nx, ny = lax.axis_size("px"), lax.axis_size("py")
    n = nx * ny
    x, y = lax.axis_index("px"), lax.axis_index("py")
    me = x * ny + y
    rows, width = 16, 128
    fields = 3 * count

    load_cur = pltpu.make_async_copy(cur_hbm, fld.at[0], load_sem.at[0])
    load_basis = pltpu.make_async_copy(basis_hbm, basis, load_sem.at[1])
    load_stiff = pltpu.make_async_copy(stiff_hbm, stiff, load_sem.at[2])
    load_cur.start()
    load_stiff.start()
    load_basis.start()

    halo_in[...] = jnp.zeros_like(halo_in)
    vh_cols[...] = jnp.zeros_like(vh_cols)
    vh_rows[...] = jnp.zeros_like(vh_rows)
    parts[...] = jnp.zeros_like(parts)

    def for_peers(act):
        def plane(px, first):
            def one(k, py):
                py = jnp.where(py == ny - 1, 0, py + 1)
                act((px, py))
                return py

            start = y if first else jnp.where(y == 0, ny - 1, y - 1)
            lax.fori_loop(first, ny, one, start, unroll=min(8, ny) if not first else 1)

        def other(k, px):
            px = jnp.where(px == nx - 1, 0, px + 1)
            plane(px, 0)
            return px

        lax.fori_loop(1, nx, other, x)
        plane(x, 1)

    barrier = pltpu.get_barrier_semaphore()

    for_peers(lambda peer: pl.semaphore_signal(barrier, inc=1, device_id=peer, device_id_type=MESH))

    row16, lane16 = iota((rows, width), 0), iota((rows, width), 1)
    row8, lane8 = iota((8, width), 0), iota((8, width), 1)

    def pack_edges(read, slot):
        packed = jnp.zeros((rows, width), jnp.float32)
        lines = jnp.zeros((8, width), jnp.float32)
        for a in range(3):
            f = read(a)
            packed = jnp.where(lane16 == a, pltpu.roll(f, a + 1, 1), packed)
            packed = jnp.where(lane16 == 3 + a, pltpu.roll(f, 3 + a, 1), packed)
            lines = jnp.where(row8 == a, jnp.broadcast_to(f[rows - 1 :, :], (8, width)), lines)
            lines = jnp.where(row8 == 3 + a, jnp.broadcast_to(f[0:1, :], (8, width)), lines)
        edge[slot, 0:rows, :] = packed
        edge[slot, rows : rows + 8, :] = lines

    def present(dx, dy):
        return (x + dx >= 0) & (x + dx < nx) & (y + dy >= 0) & (y + dy < ny)

    def halo_copy(slot, i):
        dx, dy, at, size = SENDS[i]
        first = rows if at >= COLS else (8 if dx == 1 else 0)
        return pltpu.make_async_remote_copy(
            src_ref=edge.at[slot, pl.ds(first, size), :],
            dst_ref=halo_in.at[slot, pl.ds(at, size), :],
            send_sem=halo_send.at[slot, i],
            recv_sem=halo_recv.at[slot, i],
            device_id=(x + dx, y + dy),
            device_id_type=MESH,
        )

    def vh_copy(i):
        dx, dy, at, size = SENDS[i]
        if at >= COLS:
            side = 0 if dx == 1 else 1
            src = vrows.at[side]
            dst = vh_rows.at[side, pl.ds(0, fields), :]
        else:
            side = 0 if dy == 1 else 1
            src = vcols.at[side, pl.ds(8 if dx == 1 else 0, size), :]
            dst = vh_cols.at[pl.ds(at, size), :]
        return pltpu.make_async_remote_copy(
            src_ref=src, dst_ref=dst, send_sem=vh_send.at[i], recv_sem=vh_recv.at[i],
            device_id=(x + dx, y + dy), device_id_type=MESH,
        )

    def start_all(make):
        for i, (dx, dy, _, _) in enumerate(SENDS):
            @pl.when(present(dx, dy))
            def _():
                make(i).start()

    def wait_recv_all(make):
        for i, (dx, dy, _, _) in enumerate(SENDS):
            @pl.when(present(-dx, -dy))
            def _():
                make(i).wait_recv()

    def wait_send_all(make):
        for i, (dx, dy, _, _) in enumerate(SENDS):
            @pl.when(present(dx, dy))
            def _():
                make(i).wait_send()

    load_cur.wait()
    pack_edges(lambda a: fld[0, a], 0)
    pl.semaphore_wait(barrier, n - 1)
    start_all(lambda i: halo_copy(0, i))

    load_basis.wait()
    vrows[0] = basis[pl.ds(rows - 1, fields, stride=rows), :]
    vrows[1] = basis[pl.ds(0, fields, stride=rows), :]
    last_cols = jnp.zeros((rows, width), jnp.float32)
    first_cols = jnp.zeros((rows, width), jnp.float32)
    for k in range(fields):
        f = basis[k * rows : (k + 1) * rows, :]
        last_cols = jnp.where(lane16 == k, pltpu.roll(f, (k + 1) % width, 1), last_cols)
        first_cols = jnp.where(lane16 == k, pltpu.roll(f, k, 1) if k else f, first_cols)
    vcols[0] = last_cols
    vcols[1] = first_cols
    start_all(vh_copy)
    load_stiff.wait()

    def message_copy(s, peer):
        return pltpu.make_async_remote_copy(
            src_ref=msg.at[s, pl.ds(0, 1), :],
            dst_ref=recv.at[s, pl.ds(me, 1), :],
            send_sem=msg_send.at[s],
            recv_sem=msg_recv.at[s],
            device_id=peer,
            device_id_type=MESH,
        )

    def send_message(s):
        folded = parts[pl.ds(0, width, stride=8), :]
        for j in range(1, 8):
            folded = folded + parts[pl.ds(j, width, stride=8), :]
        sums = lax.dot_general(
            jnp.ones((8, width), jnp.float32), folded, (((1,), (1,)), ((), ())),
            precision=HIGHEST, preferred_element_type=jnp.float32,
        )
        msg[s] = sums
        recv[s, pl.ds(me, 1), :] = sums[0:1]

        for_peers(lambda peer: message_copy(s, peer).start())

    def wait_message(s):
        pltpu.make_async_copy(
            recv.at[s, pl.ds(0, n - 1), :], recv.at[s, pl.ds(0, n - 1), :], msg_recv.at[s]
        ).wait()
        summed = jnp.sum(recv[s], axis=0, keepdims=True) / total_size
        return jnp.broadcast_to(summed, (8, width))

    def fold(values):
        total = values[0]
        for value in values[1:]:
            total = total + value
        return total[0:8] + total[8:16]

    def splat(row, lane):
        return jnp.broadcast_to(row[:, lane : lane + 1], (8, width))

    def twice(tile):
        return jnp.concatenate([tile, tile], axis=0)

    def stencil(s):
        left, right = halo[s, 0:16, :], halo[s, 16:32, :]

        def around(f, above, below):
            up = jnp.where(row16 == 0, jnp.broadcast_to(above, f.shape), pltpu.roll(f, 1, 0))
            down = jnp.where(row16 == rows - 1, jnp.broadcast_to(below, f.shape), pltpu.roll(f, rows - 1, 0))
            return (up, f, down)

        lefts = around(left, halo[s, 39:40, :], halo[s, 48:49, :])
        rights = around(right, halo[s, 47:48, :], halo[s, 56:57, :])
        image = [jnp.zeros((rows, width), jnp.float32) for _ in range(3)]
        for b in range(3):
            moved = around(fld[s, b], halo[s, 64 + b : 65 + b, :], halo[s, 75 + b : 76 + b, :])
            for i in range(3):
                f = moved[i]
                l = pltpu.roll(lefts[i], width - b, 1) if b else lefts[i]
                r = pltpu.roll(rights[i], width - 4 - b, 1)
                west = jnp.where(lane16 == 0, l, pltpu.roll(f, 1, 1))
                east = jnp.where(lane16 == width - 1, r, pltpu.roll(f, width - 1, 1))
                for j, g in enumerate((west, f, east)):
                    for a in range(3):
                        image[a] = image[a] + stiff[3 * i + j, a, b] * g
        return image

    wait_recv_all(lambda i: halo_copy(0, i))
    halo[0] = halo_in[0]

    rows_out = []
    betas = []
    for s in range(STEPS):
        image = stencil(s)
        for a in range(3):
            img[a] = image[a]
        if s < STEPS - 1:
            pack_edges(lambda a: img[a], s + 1)
            start_all(lambda i, s=s: halo_copy(s + 1, i))
        for m in range(count):
            part = fold([basis[(3 * m + a) * rows : (3 * m + a + 1) * rows, :] * img[a] for a in range(3)])
            for a in range(3):
                parts[(3 * m + a) * 8 : (3 * m + a + 1) * 8, :] = part
        for k in range(s + 1):
            parts[(EXTRA + k) * 8 : (EXTRA + k + 1) * 8, :] = fold([fld[k, a] * img[a] for a in range(3)])
        parts[SQUARE * 8 : SQUARE * 8 + 8, :] = fold([fld[s, a] * fld[s, a] for a in range(3)])
        send_message(s)
        if s == 0:
            wait_recv_all(vh_copy)
        if s < STEPS - 1:
            wait_recv_all(lambda i, s=s: halo_copy(s + 1, i))
        dots = wait_message(s)

        if s == 0:
            inverse = jnp.ones((8, width), jnp.float32)
        else:
            beta = jnp.sqrt(splat(dots, SQUARE) + EPSILON)
            betas.append(beta)
            inverse = 1.0 / beta
            for a in range(3):
                vector = fld[s, a] * twice(inverse)
                fld[s, a] = vector
                new_out[s - 1, a] = vector
            if s < STEPS - 1:
                halo[s] = halo[s] * inverse[0:1]
        weights = dots * inverse
        weights = jnp.where(lane8 == EXTRA + s, weights * inverse, weights)
        rows_out.append(weights)
        result = [img[a] * twice(inverse) for a in range(3)]
        for m in range(count):
            w = twice(splat(weights, 3 * m))
            for a in range(3):
                result[a] = result[a] - w * basis[(3 * m + a) * rows : (3 * m + a + 1) * rows, :]
        for k in range(s + 1):
            w = twice(splat(weights, EXTRA + k))
            for a in range(3):
                result[a] = result[a] - w * fld[k, a]
        for a in range(3):
            fld[s + 1, a] = result[a]
        if s < STEPS - 1:
            sub, lane = iota((width, width), 0), iota((width, width), 1)
            picks = (lax.rem(sub, 3) == lax.rem(lane, 3)) & (sub < 6) & (lane < fields)
            spread = jnp.where(picks, jnp.broadcast_to(weights[0:1], (width, width)), 0.0)
            cols = lax.dot_general(
                vh_cols[...], spread, (((1,), (1,)), ((), ())),
                precision=HIGHEST, preferred_element_type=jnp.float32,
            )
            lines = [
                jnp.dot(spread[0:8], vh_rows[side], precision=HIGHEST, preferred_element_type=jnp.float32)
                for side in range(2)
            ]
            ring = halo_in[s + 1] * inverse[0:1] - jnp.concatenate([cols] + lines, axis=0)
            for k in range(s + 1):
                ring = ring - splat(weights, EXTRA + k)[0:1] * halo[k]
            halo[s + 1] = ring

    parts[SQUARE * 8 : SQUARE * 8 + 8, :] = fold([fld[STEPS, a] * fld[STEPS, a] for a in range(3)])
    send_message(STEPS)
    sub, lane = iota((width, width), 0), iota((width, width), 1)
    gather = jnp.where((sub == 3 * lane) & (lane < count), 1.0, 0.0)
    gather = jnp.where((sub - EXTRA == lane - count) & (lane >= count) & (lane < count + STEPS), 1.0, gather)
    stacked = rows_out[0]
    for s in range(1, STEPS):
        stacked = jnp.where(row8 == s, rows_out[s], stacked)
    stacked = jnp.where((lane8 >= EXTRA) & (lane8 > EXTRA + row8), 0.0, stacked)
    table = jnp.dot(stacked, gather, precision=HIGHEST, preferred_element_type=jnp.float32)
    last = wait_message(STEPS)
    beta = jnp.sqrt(splat(last, SQUARE) + EPSILON)
    betas.append(beta)
    for a in range(3):
        new_out[STEPS - 1, a] = fld[STEPS, a] * twice(1.0 / beta)
    for s in range(STEPS):
        table = jnp.where((row8 == s) & (lane8 == count + 1 + s), betas[s], table)
    coef_out[...] = table[0:STEPS, 0 : count + STEPS + 1]

    for s in range(STEPS):
        wait_send_all(lambda i, s=s: halo_copy(s, i))
    wait_send_all(vh_copy)
    for s in range(STEPS + 1):
        pltpu.make_async_copy(
            recv.at[s, pl.ds(0, n - 1), :], recv.at[s, pl.ds(0, n - 1), :], msg_send.at[s]
        ).wait()


def per_device(stiffness, basis, current):
    count, _, rows, width = basis.shape
    assert (rows, width) == (16, 128) and 3 * count <= EXTRA
    n = lax.axis_size("px") * lax.axis_size("py")
    total_size = 3.0 * rows * width * n
    f32 = jnp.float32
    vmem = pltpu.VMEM
    dma = pltpu.SemaphoreType.DMA

    def body(*refs):
        kernel(count, total_size, *refs)

    new, coef = pl.pallas_call(
        body,
        out_shape=(
            vmem((STEPS, 3, rows, width), f32),
            vmem((STEPS, count + STEPS + 1), f32),
        ),
        in_specs=[pl.BlockSpec(memory_space=pl.ANY)] * 3,
        out_specs=(pl.BlockSpec(memory_space=vmem), pl.BlockSpec(memory_space=vmem)),
        scratch_shapes=[
            vmem(stiffness.shape, f32),
            vmem((3 * count * rows, width), f32),
            vmem((STEPS + 1, 3, rows, width), f32),
            vmem((3, rows, width), f32),
            vmem((STEPS, rows + 8, width), f32),
            vmem((STEPS, HALO, width), f32),
            vmem((STEPS, HALO, width), f32),
            vmem((2, rows, width), f32),
            vmem((2, 3 * count, width), f32),
            vmem((COLS, width), f32),
            vmem((2, width, width), f32),
            vmem((8 * width, width), f32),
            vmem((STEPS + 1, 8, width), f32),
            vmem((STEPS + 1, n, width), f32),
            dma((3,)),
            dma((STEPS, len(SENDS))),
            dma((STEPS, len(SENDS))),
            dma((len(SENDS),)),
            dma((len(SENDS),)),
            dma((STEPS + 1,)),
            dma((STEPS + 1,)),
        ],
        compiler_params=pltpu.CompilerParams(collective_id=0, has_side_effects=True),
        name="arnoldi",
    )(stiffness, basis.reshape(3 * count * rows, width), current)

    return new, coef


def solution(mesh):
    in_specs = (P(None, None, None, "px", "py"), P(None, None, "px", "py"), P(None, "px", "py"))
    out_specs = (P(None, None, "px", "py"), P())
    return jax.shard_map(
        per_device, mesh=mesh, in_specs=in_specs, out_specs=out_specs, check_vma=False
    )
```
